32 devices in a mesh: rows: 16 (over z, y, x), cols: 2 (over core).
Axes of the slice: x: 2, y: 2, z: 4, core: 2. Of those that a mesh axis runs over, the one named last changes fastest.
Arguments:
- eigvecs: bfloat16 [24576, 8192], P('rows', 'cols'), may hold values from -0.0390625 to 0.0390625
- eigvals: float32 [8192], P('cols'), may hold values from 0.05 to 5
- shifts: float32 [256], replicated, may hold values from 0.01 to 0.1
- rhs: bfloat16 [24576, 256], P('rows', 'cols'), may hold values from -6 to 6
- alpha_in: float32 [24576, 256], P('rows', 'cols'), may hold values from -4 to 4
Outputs:
- alpha_out: float32 [24576, 256], P('rows', 'cols')
The draws below stay inside these ranges and needn't reach their ends.
All inputs are finite; a program needn't handle non-finite values.
Results may differ from the reference program's by a relative error of at most 0.0027.
Values may be sent and summed in bfloat16 or wider, within the bound.
No kernel may reach another device: no remote copies, remote signals or barrier semaphores. Data moves between devices by JAX's collectives and lax.ppermute only.
A program may use at most 64 MiB of HBM per device.

```python
import math
import jax
import jax.numpy as jnp
from jax import lax

ROW_DEV = 1536
S = 8192
R = 256
NROWS = 24576
N_ROWS = 16


def block_scale(rng, extent, cuts, smallest, largest):
    level = 1.0
    for position, parts in cuts:
        heights = jax.random.uniform(jax.random.fold_in(jax.random.fold_in(rng, 6), position), (parts,), jnp.float32, smallest / len(cuts), largest / len(cuts))
        level = level * jnp.repeat(jnp.exp(heights), extent[position] // parts).reshape((-1,) + (1,) * (len(extent) - 1 - position))
    return level


def centred(rng, shape, deviation, reach, pieces=(), held_as=jnp.bfloat16):
    factor_of = block_scale(rng, shape, pieces, -0.22, 0.18) if pieces else 1.0
    array = jax.random.normal(rng, shape, jnp.float32) * deviation * factor_of
    return jnp.minimum(jnp.maximum(array, -reach), reach).astype(held_as)


def setup_inputs(seed: int = 0) -> dict:
    streams_of = jax.random.split(jax.random.key(seed), 6)
    eigvecs = centred(streams_of[0], (NROWS, S), NROWS ** -0.5, 0.0390625, ((0, 16), (1, 2)))
    eigvals = jnp.clip(jnp.exp(math.log(5.0) - 4.6051702 * jax.random.uniform(streams_of[1], (S,), jnp.float32) ** block_scale(streams_of[1], (S,), ((0, 2),), -0.2, 0.2)), 0.05, 5.0)
    shifts = jnp.clip(jnp.exp(jax.random.uniform(streams_of[2], (R,), jnp.float32, math.log(0.01), math.log(0.1))), 0.01, 0.1)
    rhs = centred(streams_of[3], (NROWS, R), 1.0, 6.0, ((0, 16), (1, 2)))
    alpha_in = centred(streams_of[4], (NROWS, R), 0.5, 4.0, ((0, 16), (1, 2)), jnp.float32)
    return {"eigvecs": eigvecs, "eigvals": eigvals, "shifts": shifts, "rhs": rhs, "alpha_in": alpha_in}


def reference(eigvecs, eigvals, shifts, rhs, alpha_in):
    width = eigvecs.shape[1]
    blocks = eigvecs.reshape(N_ROWS, ROW_DEV, width)
    rhs_blocks = rhs.reshape(N_ROWS, ROW_DEV, rhs.shape[1])

    def accumulate(total, pair):
        block, rhs_block = pair
        part = lax.dot_general(block, rhs_block, (((0,), (0,)), ((), ())), preferred_element_type=jnp.float32)
        return total + part, None

    start = jnp.zeros((width, rhs.shape[1]), jnp.float32)
    coeffs, _ = lax.scan(accumulate, start, (blocks, rhs_blocks))
    scaled = (coeffs / (eigvals[:, None] + shifts[None, :])).astype(jnp.bfloat16)

    def project(block):
        return jnp.dot(block, scaled, preferred_element_type=jnp.float32)

    update = lax.map(project, blocks).reshape(rhs.shape[0], rhs.shape[1])
    return alpha_in + update
```

```python
import jax
import jax.numpy as jnp
from jax import lax
from jax.experimental import pallas as pl
from jax.experimental.pallas import tpu as pltpu
from jax.sharding import PartitionSpec as P

CHUNKS = 2
LANES = 128
WIRE = jnp.float16
VMEM = pl.BlockSpec(memory_space=pltpu.VMEM)
SMEM = pl.BlockSpec(memory_space=pltpu.SMEM)
F32 = jnp.float32


def project(eigvecs, rhs_t, place, first, count, width):
    def kernel(place_ref, vec_ref, rhs_ref, out_ref):
        for i in range(count):
            block = (first + i) ^ place_ref[0]
            at = pl.multiple_of(block * width, width)
            out_ref[i] = jnp.dot(
                rhs_ref[...], vec_ref[:, pl.ds(at, width)], preferred_element_type=F32
            )

    right = rhs_t.shape[0]
    return pl.pallas_call(
        kernel,
        out_shape=jax.ShapeDtypeStruct((count, right, width), F32),
        in_specs=[SMEM, VMEM, VMEM],
        out_specs=VMEM,
        compiler_params=pltpu.CompilerParams(vmem_limit_bytes=4 << 20),
        cost_estimate=pl.CostEstimate(
            flops=2 * count * width * right * eigvecs.shape[0],
            bytes_accessed=2 * count * width * eigvecs.shape[0],
            transcendentals=0,
        ),
        name="project",
    )(place, eigvecs, rhs_t)


def expand(eigvecs, scaled, place, first, width, total=None, split=1):
    count, right = scaled.shape[0], scaled.shape[1]
    rows, piece = eigvecs.shape[0], scaled.shape[1] // split

    def kernel(place_ref, vec_ref, scaled_ref, *refs):
        acc = None
        for i in range(count):
            block = (first + i) ^ place_ref[0]
            at = pl.multiple_of(block * width, width)
            term = lax.dot_general(
                vec_ref[:, pl.ds(at, width)],
                scaled_ref[i],
                (((1,), (1,)), ((), ())),
                preferred_element_type=F32,
            )
            acc = term if acc is None else acc + term
        if total is not None:
            acc = acc + refs[0][...]
        for k, out_ref in enumerate(refs[-split:]):
            out_ref[...] = acc[:, k * piece : (k + 1) * piece]

    extra = [] if total is None else [total]
    return pl.pallas_call(
        kernel,
        out_shape=[jax.ShapeDtypeStruct((rows, piece), F32)] * split,
        in_specs=[SMEM, VMEM, VMEM] + [VMEM] * len(extra),
        out_specs=[VMEM] * split,
        compiler_params=pltpu.CompilerParams(vmem_limit_bytes=8 << 20),
        cost_estimate=pl.CostEstimate(
            flops=2 * count * width * right * rows,
            bytes_accessed=2 * count * width * rows,
            transcendentals=0,
        ),
        name="expand",
    )(place, eigvecs, scaled, *extra)


def solution(mesh):
    n_rows, n_cols = mesh.shape["rows"], mesh.shape["cols"]
    levels = n_rows.bit_length() - 1
    assert n_rows == 1 << levels
    orders = [list(range(levels)), [1, 0] + list(range(2, levels))]
    halvings = levels - 1
    blocks = 1 << halvings

    def trade(array, level):
        pairs = []
        for row in range(n_rows):
            for col in range(n_cols):
                other = row ^ (1 << orders[col % 2][level])
                pairs.append((row * n_cols + col, other * n_cols + col))
        return lax.ppermute(array, ("rows", "cols"), pairs)

    def from_next(array, k):
        return lax.ppermute(array, "cols", [((c + k) % n_cols, c) for c in range(n_cols)])

    def to_next(array, k):
        return lax.ppermute(array, "cols", [(c, (c + k) % n_cols) for c in range(n_cols)])

    def body(eigvecs, eigvals, shifts, rhs, alpha_in):
        width = eigvecs.shape[1] // CHUNKS // blocks
        fast = width % LANES == 0 and rhs.shape[1] % LANES == 0
        row, col = lax.axis_index("rows"), lax.axis_index("cols")
        place = jnp.int32(0)
        for level in range(halvings):
            even, odd = (row >> orders[0][level]) & 1, (row >> orders[1][level]) & 1
            bit = jnp.where(col % 2 == 0, even, odd)
            place = place + (bit << (halvings - 1 - level))
        place = place.astype(jnp.int32)
        where = place[None]

        own = rhs.T
        rhs_t = jnp.concatenate([own] + [from_next(own, k) for k in range(1, n_cols)], axis=0)
        right = rhs_t.shape[0]
        shift = lax.dynamic_slice(jnp.concatenate([shifts, shifts]), (col * rhs.shape[1],), (right,))

        if not fast:
            coeffs = jnp.dot(rhs_t, eigvecs, preferred_element_type=F32)
            coeffs = coeffs.reshape(right, CHUNKS, blocks, width).transpose(1, 2, 0, 3)
            order = jnp.arange(blocks, dtype=jnp.int32) ^ place
            coeffs = jnp.take(coeffs, order, axis=1)

        def piece(chunk, first, count):
            if fast:
                return project(eigvecs, rhs_t, where, chunk * blocks + first, count, width)
            return coeffs[chunk, first : first + count]

        half = blocks // 2
        pieces = []
        for chunk in range(CHUNKS):
            send = piece(chunk, half, half).astype(WIRE)
            pieces.append((send, piece(chunk, 0, half)))

        gathered = []
        for chunk in range(CHUNKS):
            send, keep = pieces[chunk]
            for level in range(halvings):
                held = keep + trade(send, level).astype(F32)
                cut = held.shape[0] // 2
                send, keep = held[cut:].astype(WIRE), held[:cut]
            mine = held.astype(WIRE)
            sums = mine.astype(F32) + trade(mine, levels - 1).astype(F32)
            at = (chunk * blocks + place) * width
            values = lax.dynamic_slice(eigvals, (at,), (width,))
            scaled = (sums / (values[None, None, :] + shift[None, :, None])).astype(jnp.bfloat16)
            for level in range(halvings - 1, 0, -1):
                scaled = jnp.concatenate([scaled, trade(scaled, level)], axis=0)
            gathered.append((scaled, trade(scaled, 0)))

        if fast:
            total = None
            for chunk in range(CHUNKS):
                for part in range(2):
                    last = chunk == CHUNKS - 1 and part == 1
                    first = chunk * blocks + part * half
                    terms = expand(
                        eigvecs, gathered[chunk][part], where, first, width, total, n_cols if last else 1
                    )
                    total = terms[0]
        else:
            scaled = jnp.stack([jnp.concatenate(g, axis=0) for g in gathered])
            scaled = jnp.take(scaled, order, axis=1)
            scaled = scaled.transpose(0, 1, 3, 2).reshape(-1, right)
            terms = jnp.split(jnp.dot(eigvecs, scaled, preferred_element_type=F32), n_cols, axis=1)
        update = terms[0]
        for k in range(1, n_cols):
            update = update + to_next(terms[k], k)
        return alpha_in + update

    return jax.shard_map(
        body,
        mesh=mesh,
        in_specs=(P("rows", "cols"), P("cols"), P(), P("rows", "cols"), P("rows", "cols")),
        out_specs=P("rows", "cols"),
        check_vma=False,
    )
```

```python
import jax
import jax.numpy as jnp
from jax import lax
from jax.experimental import pallas as pl
from jax.experimental.pallas import tpu as pltpu
from jax.sharding import PartitionSpec as P

CHUNKS = ((2, "xzy", "zyx"), (2, "xzy", "zyx"))
TAIL = 2
LANES = 128
COPIES = 4
WIRE = jnp.float16
HBM = pl.BlockSpec(memory_space=pltpu.HBM)
VMEM = pl.BlockSpec(memory_space=pltpu.VMEM)
F32 = jnp.float32


def place_in_kernel(order):
    row, col = lax.axis_index("rows"), lax.axis_index("cols")
    place = jnp.int32(0)
    for level in range(len(order[0]) - 1):
        even, odd = (row >> order[0][level]) & 1, (row >> order[1][level]) & 1
        bit = jnp.where(col % 2 == 0, even, odd).astype(jnp.int32)
        place = place + (bit << (len(order[0]) - 2 - level))
    return place


def turn(rhs):
    rows, piece = rhs[0].shape

    def kernel(*refs):
        for k in range(len(rhs)):
            refs[-1][k * piece : (k + 1) * piece, :] = refs[k][...].T

    return pl.pallas_call(
        kernel,
        out_shape=jax.ShapeDtypeStruct((piece * len(rhs), rows), rhs[0].dtype),
        in_specs=[VMEM] * len(rhs),
        out_specs=VMEM,
        compiler_params=pltpu.CompilerParams(vmem_limit_bytes=4 << 20),
        name="turn",
    )(*rhs)


def divisors_of(eigvals, shifts, n_cols, starts, widths, orders):
    right = shifts.shape[0]
    piece = right // n_cols

    def kernel(vals_ref, shifts_ref, *outs):
        col = lax.axis_index("cols")
        for k in range(n_cols):
            at = pl.multiple_of(lax.rem(col + k, n_cols) * piece, LANES)
            down = jnp.broadcast_to(shifts_ref[:, pl.ds(at, piece)], (piece, piece)).T
            for c, out_ref in enumerate(outs):
                first = pl.multiple_of(starts[c] + place_in_kernel(orders[c]) * widths[c], LANES)
                across = jnp.broadcast_to(vals_ref[:, pl.ds(first, widths[c])], (piece, widths[c]))
                out_ref[k * piece : (k + 1) * piece, :] = across + jnp.broadcast_to(down[:, :1], across.shape)

    return pl.pallas_call(
        kernel,
        out_shape=[jax.ShapeDtypeStruct((right, w), F32) for w in widths],
        in_specs=[VMEM] * 2,
        out_specs=[VMEM] * len(widths),
        compiler_params=pltpu.CompilerParams(vmem_limit_bytes=4 << 20),
        name="divisors",
    )(eigvals[None, :], shifts[None, :])


def slab_copies(vec_ref, slab_ref, sems, order, start, far):
    rows, size = slab_ref.shape
    top = place_in_kernel(order) >> (len(order[0]) - 2)
    at = pl.multiple_of(start + (top ^ far) * size, LANES)
    step = rows // COPIES
    return [
        pltpu.make_async_copy(
            vec_ref.at[pl.ds(i * step, step), pl.ds(at, size)], slab_ref.at[pl.ds(i * step, step), :], sems.at[i]
        )
        for i in range(COPIES)
    ]


def load(eigvecs, order, start, size, far, room):
    def kernel(vec_ref, slab_ref, sems):
        copies = slab_copies(vec_ref, slab_ref, sems, order, start, far)
        for copy in copies:
            copy.start()
        for copy in copies:
            copy.wait()

    return pl.pallas_call(
        kernel,
        out_shape=jax.ShapeDtypeStruct((eigvecs.shape[0], size), eigvecs.dtype),
        in_specs=[HBM],
        out_specs=VMEM,
        scratch_shapes=[pltpu.SemaphoreType.DMA((COPIES,))],
        compiler_params=pltpu.CompilerParams(vmem_limit_bytes=room),
        name="load",
    )(eigvecs)


def block_of(slab_ref, i, place, width):
    count = slab_ref.shape[1] // width
    return pl.ds(pl.multiple_of((i ^ lax.rem(place, count)) * width, LANES), width)


def project(vectors, rhs_t, order, start, far, width, size, room=None):
    rows, right = vectors.shape[0], rhs_t.shape[0]
    count = size // width

    def kernel(vec_ref, rhs_ref, out_ref, *rest):
        place = place_in_kernel(order)
        if room is None:
            for i in range(count):
                out_ref[i] = jnp.dot(
                    rhs_ref[...], vec_ref[:, block_of(vec_ref, i, place, width)], preferred_element_type=F32
                )
            return
        slab_ref, sems = rest
        copies = slab_copies(vec_ref, slab_ref, sems, order, start, far)
        for copy in copies:
            copy.start()
        step = rows // COPIES
        for k, copy in enumerate(copies):
            copy.wait()
            held = pl.ds(k * step, step)
            for i in range(count):
                term = jnp.dot(
                    rhs_ref[:, held],
                    slab_ref[held, block_of(slab_ref, i, place, width)],
                    preferred_element_type=F32,
                )
                out_ref[i] = term if k == 0 else out_ref[i] + term

    shapes = [jax.ShapeDtypeStruct((count, right, width), F32)]
    if room is not None:
        shapes.append(jax.ShapeDtypeStruct((rows, size), vectors.dtype))
    out = pl.pallas_call(
        kernel,
        out_shape=shapes,
        in_specs=[VMEM if room is None else HBM, VMEM],
        out_specs=[VMEM] * len(shapes),
        scratch_shapes=[] if room is None else [pltpu.SemaphoreType.DMA((COPIES,))],
        compiler_params=pltpu.CompilerParams(vmem_limit_bytes=room or 4 << 20),
        cost_estimate=pl.CostEstimate(
            flops=2 * size * right * rows, bytes_accessed=2 * size * rows, transcendentals=0
        ),
        name="project",
    )(vectors, rhs_t)
    return out[0], vectors if room is None else out[1]


def expand(parts, total=None, base=None, lo=0, rows=None):
    right = parts[0][1].shape[1]
    rows = rows or parts[0][0].shape[0]
    split = 1 if base is None else right // base.shape[1]
    piece = right // split
    extra = [a for a in (total, base) if a is not None]

    def kernel(*refs):
        acc = None if total is None else refs[2 * len(parts)][lo : lo + rows, :]
        for p, (_, scaled, order) in enumerate(parts):
            slab_ref, scaled_ref = refs[2 * p], refs[2 * p + 1]
            place = place_in_kernel(order)
            for i in range(scaled.shape[0]):
                term = lax.dot_general(
                    slab_ref[lo : lo + rows, block_of(slab_ref, i, place, scaled.shape[2])],
                    scaled_ref[i],
                    (((1,), (1,)), ((), ())),
                    preferred_element_type=F32,
                )
                acc = term if acc is None else acc + term
        outs = refs[2 * len(parts) + len(extra) :]
        if base is None:
            outs[0][...] = acc
            return
        outs[0][...] = acc[:, :piece] + refs[2 * len(parts) + len(extra) - 1][lo : lo + rows, :]
        for k in range(1, split):
            outs[k][...] = acc[:, k * piece : (k + 1) * piece].astype(outs[k].dtype)

    depth = sum(p[0].shape[1] for p in parts)
    flat = [a for p in parts for a in p[:2]]
    return pl.pallas_call(
        kernel,
        out_shape=[jax.ShapeDtypeStruct((rows, piece), F32 if k == 0 else jnp.bfloat16) for k in range(split)],
        in_specs=[VMEM] * (len(flat) + len(extra)),
        out_specs=[VMEM] * split,
        compiler_params=pltpu.CompilerParams(vmem_limit_bytes=12 << 20),
        cost_estimate=pl.CostEstimate(
            flops=2 * depth * right * rows, bytes_accessed=2 * depth * rows, transcendentals=0
        ),
        name="expand",
    )(*flat, *extra)


def solution(mesh):
    n_rows, n_cols = mesh.shape["rows"], mesh.shape["cols"]
    levels = n_rows.bit_length() - 1
    assert n_rows == 1 << levels
    halvings = levels - 1
    blocks = 1 << halvings

    def order_of(word):
        first = ["xyz".index(c) for c in word]
        first = [b for b in first if b < halvings]
        return first + [b for b in range(levels) if b not in first]

    def trade(array, orders, level):
        pairs = []
        for row in range(n_rows):
            for col in range(n_cols):
                other = row ^ (1 << orders[col % 2][level])
                pairs.append((row * n_cols + col, other * n_cols + col))
        return lax.ppermute(array, ("rows", "cols"), pairs)

    def from_next(array, k):
        return lax.ppermute(array, "cols", [((c + k) % n_cols, c) for c in range(n_cols)])

    def to_next(array, k):
        return lax.ppermute(array, "cols", [(c, (c + k) % n_cols) for c in range(n_cols)])

    def body(eigvecs, eigvals, shifts, rhs, alpha_in):
        shares = sum(c[0] for c in CHUNKS)
        sizes = [eigvecs.shape[1] // shares * c[0] for c in CHUNKS]
        starts = [sum(sizes[:i]) for i in range(len(sizes))]
        widths = [s // blocks for s in sizes]
        orders = [(order_of(c[1]), order_of(c[2])) for c in CHUNKS]
        fast = all(w % LANES == 0 for w in widths) and rhs.shape[1] % LANES == 0
        all_rhs = [rhs] + [from_next(rhs, k) for k in range(1, n_cols)]
        right = rhs.shape[1] * n_cols
        half = blocks // 2

        pieces, divisors = [], []
        if fast:
            first = load(eigvecs, orders[0], starts[0], sizes[0] // 2, 1, 50 << 20)
            rhs_t = turn(all_rhs)
            slabs = []
            for c, start in enumerate(starts):
                found = []
                for far in (1, 0):
                    lead = c == 0 and far
                    found.append(
                        project(
                            first if lead else eigvecs, rhs_t, orders[c], start, far, widths[c], sizes[c] // 2,
                            None if lead else 40 << 20,
                        )
                    )
                pieces.append([f[0] for f in found])
                slabs.append([f[1] for f in found])
            later = lax.optimization_barrier((eigvals, shifts, pieces[0][0]))
            pieces[0][0] = later[2]
            divisors = divisors_of(later[0], later[1], n_cols, starts, widths, orders)
        else:
            col = lax.axis_index("cols")
            shift = lax.dynamic_slice(jnp.concatenate([shifts, shifts]), (col * rhs.shape[1],), (right,))
            coeffs = jnp.dot(jnp.concatenate(all_rhs, axis=1).T, eigvecs, preferred_element_type=F32)
            swaps = []
            for c, start in enumerate(starts):
                place = place_in_kernel(orders[c])
                values = lax.dynamic_slice(eigvals, (start + place * widths[c],), (widths[c],))
                divisors.append(values[None, :] + shift[:, None])
                swaps.append(jnp.arange(blocks, dtype=jnp.int32) ^ place)
                mine = coeffs[:, start : start + sizes[c]].reshape(right, blocks, widths[c])
                mine = jnp.take(mine.transpose(1, 0, 2), swaps[c], axis=0)
                pieces.append((mine[half:], mine[:half]))

        gathered = []
        for c, start in enumerate(starts):
            send, keep = pieces[c]
            send = send.astype(WIRE)
            for level in range(halvings):
                held = keep + trade(send, orders[c], level).astype(F32)
                cut = held.shape[0] // 2
                send, keep = held[cut:].astype(WIRE), held[:cut]
            mine = held.astype(WIRE)
            sums = mine.astype(F32) + trade(mine, orders[c], levels - 1).astype(F32)
            scaled = (sums / divisors[c][None]).astype(jnp.bfloat16)
            for level in range(halvings - 1, 0, -1):
                scaled = jnp.concatenate([scaled, trade(scaled, orders[c], level)], axis=0)
            gathered.append((scaled, trade(scaled, orders[c], 0)))

        if fast:
            total = None
            for c in range(len(CHUNKS)):
                near, far = ((slabs[c][1 - k], gathered[c][k], orders[c]) for k in range(2))
                if c < len(CHUNKS) - 1:
                    total = expand([near, far], total)[0]
            total = expand([near], total)[0]
            rows = eigvecs.shape[0] // TAIL
            out = []
            for t in range(TAIL):
                terms = expand([far], total, alpha_in, t * rows, rows)
                out.append((terms[0], [to_next(terms[k], k) for k in range(1, n_cols)]))
            update = []
            for mine, others in out:
                for other in others:
                    mine = mine + other.astype(F32)
                update.append(mine)
            return jnp.concatenate(update, axis=0)
        scaled = []
        for c in range(len(CHUNKS)):
            both = jnp.take(jnp.concatenate(gathered[c], axis=0), swaps[c], axis=0)
            scaled.append(both.transpose(0, 2, 1).reshape(-1, right))
        update = jnp.dot(eigvecs, jnp.concatenate(scaled, axis=0), preferred_element_type=F32)
        terms = jnp.split(update, n_cols, axis=1)
        update = alpha_in + terms[0]
        for k in range(1, n_cols):
            update = update + to_next(terms[k], k)
        return update

    return jax.shard_map(
        body,
        mesh=mesh,
        in_specs=(P("rows", "cols"), P("cols"), P(), P("rows", "cols"), P("rows", "cols")),
        out_specs=P("rows", "cols"),
        check_vma=False,
    )
```

```python
import jax
import jax.numpy as jnp
from jax import lax
from jax.experimental import pallas as pl
from jax.experimental.pallas import tpu as pltpu
from jax.sharding import PartitionSpec as P


CHUNKS = ((2, "xyz", "yxz", "210"), (2, "yxz", "zxy", "210"))
FINISH = (0, 1)
TAIL = 1
LANES = 128
COPIES = 4
WIRE = jnp.float16
HBM = pl.BlockSpec(memory_space=pltpu.HBM)
VMEM = pl.BlockSpec(memory_space=pltpu.VMEM)
F32 = jnp.float32


def place_in_kernel(order):
    row, col = lax.axis_index("rows"), lax.axis_index("cols")
    place = jnp.int32(0)
    for level in range(len(order[0]) - 1):
        even, odd = (row >> order[0][level]) & 1, (row >> order[1][level]) & 1
        bit = jnp.where(col % 2 == 0, even, odd).astype(jnp.int32)
        place = place + (bit << (len(order[0]) - 2 - level))
    return place


def turn(rhs):
    rows, piece = rhs[0].shape

    def kernel(*refs):
        for k in range(len(rhs)):
            refs[-1][k * piece : (k + 1) * piece, :] = refs[k][...].T

    return pl.pallas_call(
        kernel,
        out_shape=jax.ShapeDtypeStruct((piece * len(rhs), rows), rhs[0].dtype),
        in_specs=[VMEM] * len(rhs),
        out_specs=VMEM,
        compiler_params=pltpu.CompilerParams(vmem_limit_bytes=4 << 20),
        name="turn",
    )(*rhs)


def divisors_of(eigvals, shifts, n_cols, starts, widths, orders):
    right = shifts.shape[0]
    piece = right // n_cols

    def kernel(vals_ref, shifts_ref, *outs):
        col = lax.axis_index("cols")
        for k in range(n_cols):
            at = pl.multiple_of(lax.rem(col + k, n_cols) * piece, LANES)
            down = jnp.broadcast_to(shifts_ref[:, pl.ds(at, piece)], (piece, piece)).T
            for c, out_ref in enumerate(outs):
                first = pl.multiple_of(starts[c] + place_in_kernel(orders[c]) * widths[c], LANES)
                across = jnp.broadcast_to(vals_ref[:, pl.ds(first, widths[c])], (piece, widths[c]))
                out_ref[k * piece : (k + 1) * piece, :] = across + jnp.broadcast_to(down[:, :1], across.shape)

    return pl.pallas_call(
        kernel,
        out_shape=[jax.ShapeDtypeStruct((right, w), F32) for w in widths],
        in_specs=[VMEM] * 2,
        out_specs=[VMEM] * len(widths),
        compiler_params=pltpu.CompilerParams(vmem_limit_bytes=4 << 20),
        name="divisors",
    )(eigvals[None, :], shifts[None, :])


def slab_copies(vec_ref, slab_ref, sems, order, start, far):
    rows, size = slab_ref.shape
    top = place_in_kernel(order) >> (len(order[0]) - 2)
    at = pl.multiple_of(start + (top ^ far) * size, LANES)
    step = rows // COPIES
    return [
        pltpu.make_async_copy(
            vec_ref.at[pl.ds(i * step, step), pl.ds(at, size)], slab_ref.at[pl.ds(i * step, step), :], sems.at[i]
        )
        for i in range(COPIES)
    ]


def load(eigvecs, order, start, size, far, room):
    def kernel(vec_ref, slab_ref, sems):
        copies = slab_copies(vec_ref, slab_ref, sems, order, start, far)
        for copy in copies:
            copy.start()
        for copy in copies:
            copy.wait()

    return pl.pallas_call(
        kernel,
        out_shape=jax.ShapeDtypeStruct((eigvecs.shape[0], size), eigvecs.dtype),
        in_specs=[HBM],
        out_specs=VMEM,
        scratch_shapes=[pltpu.SemaphoreType.DMA((COPIES,))],
        compiler_params=pltpu.CompilerParams(vmem_limit_bytes=room),
        name="load",
    )(eigvecs)


def block_of(first, i, place, width):
    return pl.ds(pl.multiple_of(first + (i ^ place) * width, LANES), width)


def project(vectors, rhs_t, order, start, far, width, count):
    rows, right = vectors.shape[0], rhs_t.shape[0]
    alone = vectors.shape[1] == count * width

    def kernel(vec_ref, rhs_ref, out_ref):
        place = place_in_kernel(order)
        place = lax.rem(place, count) if alone else place
        for i in range(count):
            at = block_of(0, i, place, width) if alone else block_of(start, i + far * count, place, width)
            out_ref[i] = jnp.dot(rhs_ref[...], vec_ref[:, at], preferred_element_type=F32)

    return pl.pallas_call(
        kernel,
        out_shape=jax.ShapeDtypeStruct((count, right, width), F32),
        in_specs=[VMEM, VMEM],
        out_specs=VMEM,
        compiler_params=pltpu.CompilerParams(vmem_limit_bytes=4 << 20),
        cost_estimate=pl.CostEstimate(
            flops=2 * count * width * right * rows, bytes_accessed=2 * count * width * rows, transcendentals=0
        ),
        name="project",
    )(vectors, rhs_t)


def expand(eigvecs, parts, total=None, base=None, lo=0, rows=None):
    right = parts[0][0].shape[1]
    rows = rows or eigvecs.shape[0]
    split = 1 if base is None else right // base.shape[1]
    piece = right // split
    extra = [a for a in (total, base) if a is not None]

    def kernel(vec_ref, *refs):
        acc = None if total is None else refs[len(parts)][lo : lo + rows, :]
        for scaled_ref, (scaled, order, start, held) in zip(refs, parts):
            place = place_in_kernel(order)
            for i in range(scaled.shape[0]):
                term = lax.dot_general(
                    vec_ref[lo : lo + rows, block_of(start, held[i], place, scaled.shape[2])],
                    scaled_ref[i],
                    (((1,), (1,)), ((), ())),
                    preferred_element_type=F32,
                )
                acc = term if acc is None else acc + term
        outs = refs[len(parts) + len(extra) :]
        if base is None:
            outs[0][...] = acc
            return
        outs[0][...] = acc[:, :piece] + refs[len(parts) + len(extra) - 1][lo : lo + rows, :]
        for k in range(1, split):
            outs[k][...] = acc[:, k * piece : (k + 1) * piece].astype(outs[k].dtype)

    depth = sum(p[0].shape[0] * p[0].shape[2] for p in parts)
    return pl.pallas_call(
        kernel,
        out_shape=[jax.ShapeDtypeStruct((rows, piece), F32 if k == 0 else jnp.bfloat16) for k in range(split)],
        in_specs=[VMEM] * (1 + len(parts) + len(extra)),
        out_specs=[VMEM] * split,
        compiler_params=pltpu.CompilerParams(vmem_limit_bytes=12 << 20),
        cost_estimate=pl.CostEstimate(
            flops=2 * depth * right * rows, bytes_accessed=2 * depth * rows, transcendentals=0
        ),
        name="expand",
    )(eigvecs, *[p[0] for p in parts], *extra)


def solution(mesh):
    n_rows, n_cols = mesh.shape["rows"], mesh.shape["cols"]
    levels = n_rows.bit_length() - 1
    assert n_rows == 1 << levels
    halvings = levels - 1
    blocks = 1 << halvings

    def order_of(word):
        first = ["xyz".index(c) for c in word]
        first = [b for b in first if b < halvings]
        return first + [b for b in range(levels) if b not in first]

    def trade(array, orders, level):
        pairs = []
        for row in range(n_rows):
            for col in range(n_cols):
                other = row ^ (1 << orders[col % 2][level])
                pairs.append((row * n_cols + col, other * n_cols + col))
        return lax.ppermute(array, ("rows", "cols"), pairs)

    def from_next(array, k):
        return lax.ppermute(array, "cols", [((c + k) % n_cols, c) for c in range(n_cols)])

    def to_next(array, k):
        return lax.ppermute(array, "cols", [(c, (c + k) % n_cols) for c in range(n_cols)])

    def body(eigvecs, eigvals, shifts, rhs, alpha_in):
        shares = sum(c[0] for c in CHUNKS)
        sizes = [eigvecs.shape[1] // shares * c[0] for c in CHUNKS]
        starts = [sum(sizes[:i]) for i in range(len(sizes))]
        widths = [s // blocks for s in sizes]
        orders = [(order_of(c[1]), order_of(c[2])) for c in CHUNKS]
        fast = all(w % LANES == 0 for w in widths) and rhs.shape[1] % LANES == 0
        all_rhs = [rhs] + [from_next(rhs, k) for k in range(1, n_cols)]
        right = rhs.shape[1] * n_cols
        half = blocks // 2

        pieces, divisors = [], []
        if fast:
            first = load(eigvecs, orders[0], starts[0], sizes[0] // 2, 1, 46 << 20)
            rhs_t = turn(all_rhs)
            for c, start in enumerate(starts):
                found = []
                for f in (1, 0):
                    found.append(
                        project(first if c == 0 and f else eigvecs, rhs_t, orders[c], start, f, widths[c], half)
                    )
                pieces.append(found)
            later = lax.optimization_barrier((eigvals, shifts, pieces[0][0]))
            pieces[0][0] = later[2]
            divisors = divisors_of(later[0], later[1], n_cols, starts, widths, orders)
        else:
            col = lax.axis_index("cols")
            shift = lax.dynamic_slice(jnp.concatenate([shifts, shifts]), (col * rhs.shape[1],), (right,))
            coeffs = jnp.dot(jnp.concatenate(all_rhs, axis=1).T, eigvecs, preferred_element_type=F32)
            swaps = []
            for c, start in enumerate(starts):
                place = place_in_kernel(orders[c])
                values = lax.dynamic_slice(eigvals, (start + place * widths[c],), (widths[c],))
                divisors.append(values[None, :] + shift[:, None])
                swaps.append(jnp.arange(blocks, dtype=jnp.int32) ^ place)
                mine = coeffs[:, start : start + sizes[c]].reshape(right, blocks, widths[c])
                mine = jnp.take(mine.transpose(1, 0, 2), swaps[c], axis=0)
                pieces.append((mine[half:], mine[:half]))

        gathered = []
        for c, start in enumerate(starts):
            send, keep = pieces[c]
            send, cut = send.astype(WIRE), send.shape[0] // 2
            high = keep[cut:] + trade(send[cut:], orders[c], 0).astype(F32)
            low = trade(send[:cut], orders[c], 0).astype(F32)
            send, keep = high.astype(WIRE), keep[:cut] + low
            for level in range(1, halvings):
                held = keep + trade(send, orders[c], level).astype(F32)
                cut = held.shape[0] // 2
                send, keep = held[cut:].astype(WIRE), held[:cut]
            mine = held.astype(WIRE)
            sums = mine.astype(F32) + trade(mine, orders[c], halvings).astype(F32)
            scaled = (sums / divisors[c][None]).astype(jnp.bfloat16)
            held = [0]
            back = [int(n) for n in CHUNKS[c][3]]
            back = back if len(back) == halvings else list(range(halvings))[::-1]
            for level in back[:-1]:
                other = trade(scaled, orders[c], level)
                start = scaled
                scaled = jnp.concatenate([scaled, other], axis=0)
                held = held + [q | 1 << (halvings - 1 - level) for q in held]
            beyond = [q | 1 << (halvings - 1 - back[-1]) for q in held]
            cut = len(held) // 2
            far = (trade(start, orders[c], back[-1]), trade(other, orders[c], back[-1]))
            gathered.append(((scaled, held), (far[0], beyond[:cut]), (far[1], beyond[cut:])))

        if fast:
            parts = [[(g[0], orders[c], starts[c], g[1]) for g in gathered[c]] for c in FINISH]
            total = expand(eigvecs, [p[0] for p in parts])[0]
            for p in parts[:-1]:
                total = expand(eigvecs, p[1:], total)[0]
            total = expand(eigvecs, [parts[-1][1]], total)[0]
            rows = eigvecs.shape[0] // TAIL
            out = []
            for t in range(TAIL):
                terms = expand(eigvecs, [parts[-1][2]], total, alpha_in, t * rows, rows)
                out.append((terms[0], [to_next(terms[k], k) for k in range(1, n_cols)]))
            update = []
            for mine, others in out:
                for other in others:
                    mine = mine + other.astype(F32)
                update.append(mine)
            return jnp.concatenate(update, axis=0)
        scaled = []
        for c in range(len(CHUNKS)):
            both = jnp.concatenate([g[0] for g in gathered[c]], axis=0)
            held = sum((g[1] for g in gathered[c]), [])
            both = jnp.stack([both[held.index(q)] for q in range(blocks)])
            both = jnp.take(both, swaps[c], axis=0)
            scaled.append(both.transpose(0, 2, 1).reshape(-1, right))
        update = jnp.dot(eigvecs, jnp.concatenate(scaled, axis=0), preferred_element_type=F32)
        terms = jnp.split(update, n_cols, axis=1)
        update = alpha_in + terms[0]
        for k in range(1, n_cols):
            update = update + to_next(terms[k], k)
        return update

    return jax.shard_map(
        body,
        mesh=mesh,
        in_specs=(P("rows", "cols"), P("cols"), P(), P("rows", "cols"), P("rows", "cols")),
        out_specs=P("rows", "cols"),
        check_vma=False,
    )
```
